128 devices in a mesh: inst: 4 (over x_lo, core), space: 32 (over y, x_hi, z).
Axes of the slice: x: 4 (x_hi: 2, x_lo: 2; x = x_hi * 2 + x_lo), y: 4, z: 4, core: 2. Of those that a mesh axis runs over, the one named last changes fastest.
Arguments:
- adjoint_old: float32 [8, 6, 2048, 512], P('inst', None, 'space'), may hold values from -6 to 6
- source_term: float32 [8, 6, 2048, 512], P('inst', None, 'space'), may hold values from -6 to 6
- face_stream: float32 [8, 2048, 512], P('inst', 'space'), may hold values from 0.2 to 1
- face_pitch: float32 [8, 2048, 512], P('inst', 'space'), may hold values from 0.2 to 1
- diag_scale: float32 [8, 2048, 512], P('inst', 'space'), may hold values from 0.1 to 0.4
- volume: float32 [2048, 512], P('space'), may hold values from 0.5 to 2
- face_blocks: float32 [4, 6, 6], replicated, may hold values from -2.5 to 2.5
- diag_inverse: float32 [8, 6, 6], P('inst')
- periodic_block: float32 [6, 6], replicated, may hold values from -2.5 to 2.5
- frequency: float32 [1], replicated, may hold values from 0.5 to 2
- phase_shift: int32 [1], replicated, may hold values from 1 to 7
- periodic_cells: int32 [32, 32, 128], P('space'), may hold values from 0 to 32767
- periodic_targets: int32 [32, 32, 128], P(None, 'space'), may hold values from 0 to 32767
- periodic_weights: float32 [32, 32, 128], P('space'), may hold values from 0.5 to 1.5
- periodic_counts: int32 [32, 32], P('space'), may hold values from 0 to 128, as said below
Outputs:
- adjoint_new: float32 [8, 6, 2048, 512], P('inst', None, 'space')
- residual: float32 [8, 6, 2048, 512], P('inst', None, 'space')
The draws below stay inside these ranges and needn't reach their ends.
Inputs may be any that keep to these rules, and one draw needn't show every extreme that they name: `periodic_counts`: each partition's row has one peer with 128 live faces, and one partition receives 128 live faces from every partition. `periodic_cells`: local cell indices in the sending partition. `periodic_targets`: local cell indices in the receiving partition.
All inputs are finite; a program needn't handle non-finite values.
Results may differ from the reference program's by a relative error of at most 0.0001.
Values sent between devices are 32-bit elements; how exact they have to be, the bound alone decides.
No kernel may reach another device: no remote copies, remote signals or barrier semaphores. Data moves between devices by JAX's collectives and lax.ppermute only.
A program may use at most 128 MiB of HBM per device.

```python
import math
import jax
import jax.numpy as jnp
from jax import lax

VARS = 6
CI = 64
NJ = 512
PSLOT = 128
SWEEPS = 2
INSTANCES = 8
NI = 2048
N_SPACE = 32


def draw_diag_inverse(key, part):
    noise = jax.random.normal(key, (INSTANCES, VARS, VARS), jnp.float32) * 0.5
    return jnp.eye(VARS, dtype=jnp.float32)[None] + noise / math.sqrt(VARS)


def draw_periodic_counts(key, part):
    first = jax.random.fold_in(key, 11)
    second = jax.random.fold_in(key, 12)
    third = jax.random.fold_in(key, 13)
    counts = jax.random.randint(first, (N_SPACE, N_SPACE), 0, PSLOT + 1)
    peers = jax.random.permutation(second, N_SPACE)
    counts = counts.at[jnp.arange(N_SPACE), peers].set(PSLOT)
    column = jax.random.randint(third, (), 0, N_SPACE)
    counts = counts.at[:, column].set(PSLOT)
    return counts.astype(jnp.int32)


def with_ends(drawn, stream_key, low, largest):
    longest = drawn.shape.index(max(drawn.shape))
    spots = []
    for shift in (0, 1):
        where = [jax.random.randint(jax.random.fold_in(stream_key, axis), (), 0, length) for axis, length in enumerate(drawn.shape)]
        where[longest] = (where[longest] + shift) % drawn.shape[longest]
        spots.append(tuple(where))
    return drawn.at[spots[0]].set(low).at[spots[1]].set(largest)


def level_of(key, shape, cuts, least, top_value):
    loudness, own = 1.0, jax.random.fold_in(key, 6)
    for position, blocks in cuts:
        draws = jnp.exp(jax.random.uniform(jax.random.fold_in(own, position), (blocks,), jnp.float32, least / len(cuts), top_value / len(cuts)))
        loudness = loudness * jnp.repeat(draws, shape[position] // blocks).reshape([-1 if axis == position else 1 for axis in range(len(shape))])
    return loudness


def gaussian(rng, extent, width, bound, cuts=(), kind=jnp.bfloat16):
    loudness = level_of(rng, extent, cuts, -0.22, 0.18) if cuts else 1.0
    array = jax.random.normal(rng, extent, jnp.float32) * width * loudness
    return jnp.minimum(jnp.maximum(array, -bound), bound).astype(kind)


def setup_inputs(seed: int = 0) -> dict:
    streams_of = jax.random.split(jax.random.key(seed), 16)
    adjoint_old = gaussian(streams_of[0], (INSTANCES, VARS, NI, NJ), 1.0, 6.0, ((0, 4), (2, 32)), jnp.float32)
    source_term = gaussian(streams_of[1], (INSTANCES, VARS, NI, NJ), 1.0, 6.0, ((0, 4), (2, 32)), jnp.float32)
    face_stream = jnp.clip(0.2 + 0.8 * jax.random.uniform(streams_of[2], (INSTANCES, NI, NJ), jnp.float32) ** level_of(streams_of[2], (INSTANCES, NI, NJ), ((0, 4), (1, 32)), -0.2, 0.2), 0.2, 1.0)
    face_pitch = jnp.clip(0.2 + 0.8 * jax.random.uniform(streams_of[3], (INSTANCES, NI, NJ), jnp.float32) ** level_of(streams_of[3], (INSTANCES, NI, NJ), ((0, 4), (1, 32)), -0.2, 0.2), 0.2, 1.0)
    diag_scale = jnp.clip(jnp.exp(math.log(0.4) - 1.3862944 * jax.random.uniform(streams_of[4], (INSTANCES, NI, NJ), jnp.float32) ** level_of(streams_of[4], (INSTANCES, NI, NJ), ((0, 4), (1, 32)), -0.2, 0.2)), 0.1, 0.4)
    volume = jnp.clip(jnp.exp(math.log(2.0) - 1.3862944 * jax.random.uniform(streams_of[5], (NI, NJ), jnp.float32) ** level_of(streams_of[5], (NI, NJ), ((0, 32),), -0.2, 0.2)), 0.5, 2.0)
    face_blocks = gaussian(streams_of[6], (4, VARS, VARS), VARS ** -0.5, 2.5, (), jnp.float32)
    diag_inverse = draw_diag_inverse(jax.random.fold_in(streams_of[15], 71), 0)
    periodic_block = gaussian(streams_of[8], (VARS, VARS), VARS ** -0.5, 2.5, (), jnp.float32)
    frequency = jnp.clip(jnp.exp(jax.random.uniform(streams_of[9], (1,), jnp.float32, math.log(0.5), math.log(2.0))), 0.5, 2.0)
    phase_shift = jax.random.randint(streams_of[10], (1,), 1, INSTANCES).astype(jnp.int32)
    periodic_cells = with_ends(jax.random.randint(streams_of[11], (N_SPACE, N_SPACE, PSLOT), 0, CI * NJ), jax.random.fold_in(streams_of[11], 1), 0, (CI * NJ) - 1).astype(jnp.int32)
    periodic_targets = with_ends(jax.random.randint(streams_of[12], (N_SPACE, N_SPACE, PSLOT), 0, CI * NJ), jax.random.fold_in(streams_of[12], 1), 0, (CI * NJ) - 1).astype(jnp.int32)
    periodic_weights = jnp.clip(0.5 + 1.0 * jax.random.uniform(streams_of[13], (N_SPACE, N_SPACE, PSLOT), jnp.float32) ** level_of(streams_of[13], (N_SPACE, N_SPACE, PSLOT), ((0, 32),), -0.2, 0.2), 0.5, 1.5)
    periodic_counts = draw_periodic_counts(jax.random.fold_in(streams_of[15], 71), 0)
    return dict(adjoint_old=adjoint_old, source_term=source_term, face_stream=face_stream, face_pitch=face_pitch, diag_scale=diag_scale, volume=volume, face_blocks=face_blocks, diag_inverse=diag_inverse, periodic_block=periodic_block, frequency=frequency, phase_shift=phase_shift, periodic_cells=periodic_cells, periodic_targets=periodic_targets, periodic_weights=periodic_weights, periodic_counts=periodic_counts)


def spectral_matrix():
    order = jnp.arange(INSTANCES, dtype=jnp.int32)
    offset = order[:, None] - order[None, :]
    parity = jnp.where(offset % 2 == 0, 1.0, -1.0)
    nonzero = offset != 0
    angle = math.pi * offset / INSTANCES
    safe = jnp.where(nonzero, angle, 1.0)
    return jnp.where(nonzero, 0.5 * parity * jnp.cos(safe) / jnp.sin(safe), 0.0).astype(jnp.float32)


def transposed(block, field):
    return jnp.einsum("vu,kvij->kuij", block, field, precision=lax.Precision.HIGHEST)


def neighbours(adjoint, face_stream, face_pitch, face_blocks):
    zero_row = jnp.zeros_like(adjoint[:, :, :1])
    weighted = face_stream[:, None] * adjoint
    from_lower = jnp.concatenate([zero_row, weighted[:, :, :-1]], axis=2)
    from_upper = face_stream[:, None] * jnp.concatenate([adjoint[:, :, 1:], zero_row], axis=2)
    zero_col = jnp.zeros_like(adjoint[..., :1])
    side = face_pitch[:, None] * adjoint
    from_left = jnp.concatenate([zero_col, side[..., :-1]], axis=3)
    from_right = face_pitch[:, None] * jnp.concatenate([adjoint[..., 1:], zero_col], axis=3)
    return (transposed(face_blocks[0], from_lower) + transposed(face_blocks[1], from_upper)
            + transposed(face_blocks[2], from_left) + transposed(face_blocks[3], from_right))


def reference(adjoint_old, source_term, face_stream, face_pitch, diag_scale, volume, face_blocks, diag_inverse,
              periodic_block, frequency, phase_shift, periodic_cells, periodic_targets, periodic_weights,
              periodic_counts):
    cells = CI * NJ
    flat = adjoint_old.reshape(INSTANCES, VARS, N_SPACE, cells)
    index = periodic_cells.reshape(N_SPACE, N_SPACE * PSLOT)
    picked = jnp.take_along_axis(flat, index[None, None], axis=3)
    slots = jnp.arange(PSLOT, dtype=jnp.int32)
    live = slots[None, None, :] < periodic_counts[:, :, None]
    weights = jnp.where(live, periodic_weights, 0.0).reshape(N_SPACE, N_SPACE * PSLOT)
    picked = jnp.einsum("vu,gvpr->gupr", periodic_block, picked, precision=lax.Precision.HIGHEST) * weights
    picked = jnp.roll(picked, phase_shift[0], axis=0)
    owner = jnp.arange(N_SPACE, dtype=jnp.int32)[None, :, None] * cells
    target = (owner + periodic_targets).reshape(-1)
    periodic = jnp.zeros((INSTANCES, VARS, N_SPACE * cells), adjoint_old.dtype)
    periodic = periodic.at[:, :, target].add(picked.reshape(INSTANCES, VARS, -1))
    periodic = periodic.reshape(INSTANCES, VARS, NI, NJ)
    dmat = spectral_matrix()
    adjoint = adjoint_old
    residual = adjoint_old
    for sweep_index in range(SWEEPS):
        coupling = frequency[0] * volume * jnp.einsum("mg,mvij->gvij", dmat, adjoint,
                                                      precision=lax.Precision.HIGHEST)
        residual = source_term - neighbours(adjoint, face_stream, face_pitch, face_blocks) - coupling - periodic
        adjoint = diag_scale[:, None] * jnp.einsum("guv,gvij->guij", diag_inverse, residual,
                                                   precision=lax.Precision.HIGHEST)
    return adjoint, residual
```

```python
import math

import jax
import jax.numpy as jnp
import numpy as np
from jax import lax
from jax.experimental import pallas as pl
from jax.experimental.pallas import tpu as pltpu
from jax.sharding import PartitionSpec as P

INSTANCES = 8
BLK = 8
SEND = ((0, 2), (2, 6))
PIECES = ((0, 2), (2, 2), (4, 2), (6, 2))
VMEM = 48 * 1024 * 1024
HIGH = lax.Precision.HIGHEST


def coef(k):
    k = k % INSTANCES
    if k in (0, 4):
        return 0.0
    return 0.5 * (-1.0) ** k / math.tan(math.pi * k / INSTANCES)


def partner(value, bit):
    return lax.ppermute(value, "inst", [(i, i ^ bit) for i in range(4)])


def from_behind(value, steps):
    count = lax.axis_size("space")
    first, last = max(0, -steps), min(count, count - steps)
    return lax.ppermute(value, "space", [(s, s + steps) for s in range(first, last)])


def smem():
    return pl.BlockSpec(memory_space=pltpu.SMEM)


def params():
    return pltpu.CompilerParams(vmem_limit_bytes=VMEM)


def split(x):
    hi = x.astype(jnp.bfloat16)
    lo = (x - hi.astype(jnp.float32)).astype(jnp.bfloat16)
    return hi, lo


def pick_kernel(pb_ref, cnt_ref, a_ref, fs_ref, cell_ref, wt_ref, out_ref, lo_ref, hi_ref, tab):
    step = pl.program_id(0)

    @pl.when(step == 0)
    def _():
        for f in range(12):
            hi, lo = split(a_ref[f])
            tab[f * 64 : f * 64 + 64, 0:512] = hi
            tab[f * 64 : f * 64 + 64, 512:1024] = lo
        for f in range(12):
            lo_ref[f : f + 1, :] = fs_ref[f // 6, 7:8, :] * a_ref[f, 63:64, :]
            hi_ref[f : f + 1, :] = a_ref[f, 0:1, :]

    cells = cell_ref[...]
    cols = lax.bitwise_and(cells, 511)
    rows = lax.shift_right_logical(cells, 9)
    lane = lax.broadcasted_iota(jnp.int32, (512, 128), 0)
    sub = lax.broadcasted_iota(jnp.int32, (64, 128), 0)
    slot = lax.broadcasted_iota(jnp.int32, (1, 128), 1)
    for half in range(2):
        hot = jnp.concatenate(
            [
                jnp.where(lane == cols[q : q + 1, :], 1.0, 0.0).astype(jnp.bfloat16)
                for q in range(4 * half, 4 * half + 4)
            ],
            axis=1,
        )
        part = jnp.dot(tab[...], jnp.concatenate([hot, hot], axis=0), preferred_element_type=jnp.float32)
        for k in range(4):
            q = 4 * half + k
            mask = sub == rows[q : q + 1, :]
            weight = jnp.where(slot < cnt_ref[0, step * 8 + q], wt_ref[q : q + 1, :], 0.0)
            for g in range(2):
                got = []
                for v in range(6):
                    f = g * 6 + v
                    mine = part[f * 64 : f * 64 + 64, k * 128 : k * 128 + 128]
                    got.append(jnp.sum(jnp.where(mask, mine, 0.0), axis=0, keepdims=True))
                for u in range(6):
                    total = pb_ref[0, u] * got[0]
                    for v in range(1, 6):
                        total = total + pb_ref[v, u] * got[v]
                    out_ref[g, u, q : q + 1, :] = total * weight


def pick(block, counts, a, fs, cells, weights):
    return pl.pallas_call(
        pick_kernel,
        name="pick",
        grid=(4,),
        in_specs=[
            smem(),
            smem(),
            pl.BlockSpec((12, 64, 512), lambda i: (0, 0, 0)),
            pl.BlockSpec((2, 8, 512), lambda i: (0, 7, 0)),
            pl.BlockSpec((8, 128), lambda i: (i, 0)),
            pl.BlockSpec((8, 128), lambda i: (i, 0)),
        ],
        out_specs=[
            pl.BlockSpec((2, 6, 8, 128), lambda i: (0, 0, i, 0)),
            pl.BlockSpec((12, 512), lambda i: (0, 0)),
            pl.BlockSpec((12, 512), lambda i: (0, 0)),
        ],
        out_shape=[
            jax.ShapeDtypeStruct((2, 6, 32, 128), jnp.float32),
            jax.ShapeDtypeStruct((12, 512), jnp.float32),
            jax.ShapeDtypeStruct((12, 512), jnp.float32),
        ],
        scratch_shapes=[pltpu.VMEM((768, 1024), jnp.bfloat16)],
        compiler_params=params(),
    )(block, counts, a, fs, cells, weights)


def place_kernel(row0, rows_here, val_ref, tgt_ref, out_ref):
    step = pl.program_id(0)
    cells = tgt_ref[...]
    cols = lax.bitwise_and(cells, 511)
    rows = lax.shift_right_logical(cells, 9) - row0
    lane = lax.broadcasted_iota(jnp.int32, (512, 128), 0)
    sub = lax.broadcasted_iota(jnp.int32, (rows_here, 128), 0)
    hot = jnp.concatenate(
        [jnp.where(lane == cols[p : p + 1, :], 1.0, 0.0).astype(jnp.bfloat16) for p in range(8)], axis=1
    )
    highs, lows = [], []
    for p in range(8):
        mask = sub == rows[p : p + 1, :]
        spread = [jnp.where(mask, val_ref[p, f : f + 1, :], 0.0) for f in range(12)]
        hi, lo = split(jnp.concatenate(spread, axis=0))
        highs.append(hi)
        lows.append(lo)
    dims = (((1,), (1,)), ((), ()))
    total = lax.dot_general(
        jnp.concatenate(highs + lows, axis=1),
        jnp.concatenate([hot, hot], axis=1),
        dims,
        preferred_element_type=jnp.float32,
    )
    total = total.reshape(12, rows_here, 512)

    @pl.when(step == 0)
    def _():
        out_ref[...] = total

    @pl.when(step > 0)
    def _():
        out_ref[...] += total


def place(values, targets, piece):
    b0, nb = piece
    rows = nb * BLK

    def kernel(*refs):
        place_kernel(b0 * BLK, rows, *refs)

    return pl.pallas_call(
        kernel,
        name="place",
        grid=(4,),
        in_specs=[
            pl.BlockSpec((8, 12, 128), lambda i: (i, 0, 0)),
            pl.BlockSpec((8, 128), lambda i: (i, 0)),
        ],
        out_specs=pl.BlockSpec((12, rows, 512), lambda i: (0, 0, 0)),
        out_shape=jax.ShapeDtypeStruct((12, rows, 512), jnp.float32),
        compiler_params=params(),
    )(values, targets)


def own_terms(core, j):
    own = [coef(i - j) for i in range(2)]
    sib = [(coef(2 + i - j), coef(-2 + i - j)) for i in range(2)]
    return own, [jnp.where(core == 0, jnp.float32(e), jnp.float32(o)) for e, o in sib]


def far_terms(core, j):
    par = [coef(4 + i - j) for i in range(2)]
    sp = [(coef(6 + i - j), coef(2 + i - j)) for i in range(2)]
    return par, [jnp.where(core == 0, jnp.float32(e), jnp.float32(o)) for e, o in sp]


def weighted(terms, fields):
    total = None
    for c, x in zip(terms, fields):
        if isinstance(c, float) and c == 0.0:
            continue
        total = c * x if total is None else total + c * x
    return total


def sweep_kernel(
    last_sweep, b0, nb, fb_ref, di_ref, fr_ref, cur, prev, nxt, hlo, hhi, src, fs_ref, fsp_ref, fp_ref, dg_ref,
    vol_ref, per_ref, sib, *rest,
):
    step = pl.program_id(0)
    blk = b0 + step
    core = lax.rem(lax.axis_index("inst"), 2)
    if last_sweep:
        (far,), rest = rest[:1], rest[1:]
        out, res_out = rest[-2:]
    else:
        (par, sp), rest = rest[:2], rest[2:]
        out, piece, edge_lo, edge_hi = rest[-4:]
    row = lax.broadcasted_iota(jnp.int32, (BLK, 512), 0)
    col = lax.broadcasted_iota(jnp.int32, (BLK, 512), 1)
    top, bottom = row == 0, row == BLK - 1
    left, right = col == 0, col == 511
    fv = fr_ref[0] * vol_ref[...]
    for g in range(2):
        fs, fp, dg = fs_ref[g], fp_ref[g], dg_ref[g]
        fs_before = fsp_ref[g, BLK - 1 : BLK, :]
        own_w, sib_w = own_terms(core, g)
        if not last_sweep:
            par_w, sp_w = far_terms(core, g)
        r = [src[g, u] - per_ref[g * 6 + u] for u in range(6)]
        for v in range(6):
            f = g * 6 + v
            a = cur[g, v]
            before = jnp.where(blk == 0, hlo[f : f + 1, :], fs_before * prev[g, v, BLK - 1 : BLK, :])
            after = jnp.where(blk == 7, hhi[f : f + 1, :], nxt[g, v, 0:1, :])
            lower = jnp.where(top, before, pltpu.roll(fs * a, 1, 0))
            upper = fs * jnp.where(bottom, after, pltpu.roll(a, BLK - 1, 0))
            lft = jnp.where(left, 0.0, pltpu.roll(fp * a, 1, 1))
            rgt = fp * jnp.where(right, 0.0, pltpu.roll(a, 511, 1))
            for u in range(6):
                r[u] = r[u] - (
                    (fb_ref[0, v, u] * lower + fb_ref[1, v, u] * upper)
                    + (fb_ref[2, v, u] * lft + fb_ref[3, v, u] * rgt)
                )
            mixed = weighted(own_w + sib_w, [cur[0, v], cur[1, v], sib[0, v], sib[1, v]])
            if last_sweep:
                mixed = mixed + far[g, v]
            else:
                mixed = mixed + weighted(par_w + sp_w, [par[0, v], par[1, v], sp[0, v], sp[1, v]])
            r[v] = r[v] - fv * mixed
        for u in range(6):
            total = di_ref[g, u, 0] * r[0]
            for v in range(1, 6):
                total = total + di_ref[g, u, v] * r[v]
            new = dg * total
            out[g, u] = new
            if last_sweep:
                res_out[g, u] = r[u]
            else:
                piece[g, u] = new
                f = g * 6 + u

                @pl.when(blk == 7)
                def _(new=new, f=f, fs=fs):
                    edge_lo[f : f + 1, :] = (fs * new)[BLK - 1 : BLK, :]

                @pl.when(blk == 0)
                def _(new=new, f=f):
                    edge_hi[f : f + 1, :] = new[0:1, :]


def sweep(last_sweep, piece, common, a, halo, per, sib, sib_b0, far, far_b0, into):
    b0, nb = piece
    fb, di, fr, src, fs, fp, dg, vol = common
    big = (2, 6, BLK, 512)
    small = (2, BLK, 512)

    def at(off):
        return lambda i: (0, 0, off + i, 0)

    def at3(off):
        return lambda i: (0, off + i, 0)

    halo_spec = pl.BlockSpec((12, 512), lambda i: (0, 0))
    specs = [
        smem(), smem(), smem(),
        pl.BlockSpec(big, at(b0)),
        pl.BlockSpec(big, lambda i: (0, 0, jnp.maximum(b0 + i - 1, 0), 0)),
        pl.BlockSpec(big, lambda i: (0, 0, jnp.minimum(b0 + i + 1, 7), 0)),
        halo_spec, halo_spec,
        pl.BlockSpec(big, at(b0)),
        pl.BlockSpec(small, at3(b0)),
        pl.BlockSpec(small, lambda i: (0, jnp.maximum(b0 + i - 1, 0), 0)),
        pl.BlockSpec(small, at3(b0)),
        pl.BlockSpec(small, at3(b0)),
        pl.BlockSpec((BLK, 512), lambda i: (b0 + i, 0)),
        pl.BlockSpec((12, BLK, 512), at3(0)),
        pl.BlockSpec(big, at(sib_b0)),
    ]
    args = [fb, di, fr, a, a, a, halo[0], halo[1], src, fs, fs, fp, dg, vol, per, sib]
    for x in far:
        specs.append(pl.BlockSpec(big, at(far_b0)))
        args.append(x)
    full = jax.ShapeDtypeStruct((2, 6, 64, 512), jnp.float32)
    out_specs = [pl.BlockSpec(big, at(b0))]
    out_shape = [full]
    if last_sweep:
        out_specs.append(pl.BlockSpec(big, at(b0)))
        out_shape.append(full)
    else:
        out_specs += [pl.BlockSpec(big, at(0)), halo_spec, halo_spec]
        out_shape += [
            jax.ShapeDtypeStruct((2, 6, nb * BLK, 512), jnp.float32),
            jax.ShapeDtypeStruct((12, 512), jnp.float32),
            jax.ShapeDtypeStruct((12, 512), jnp.float32),
        ]
    aliases = {}
    if into is not None:
        for k, x in enumerate(into):
            aliases[len(args)] = k
            specs.append(pl.BlockSpec(memory_space=pl.ANY))
            args.append(x)

    def kernel(*refs):
        sweep_kernel(last_sweep, b0, nb, *refs)

    return pl.pallas_call(
        kernel,
        name="sweep2" if last_sweep else "sweep1",
        grid=(nb,),
        in_specs=specs,
        out_specs=out_specs,
        out_shape=out_shape,
        input_output_aliases=aliases,
        compiler_params=params(),
    )(*args)


def combine_kernel(own, sib, out):
    core = lax.rem(lax.axis_index("inst"), 2)
    for j in range(2):
        own_w, sib_w = far_terms(core, j)
        for v in range(6):
            out[j, v] = weighted(own_w + sib_w, [own[0, v], own[1, v], sib[0, v], sib[1, v]])


def combine(own, sib):
    big = (2, 6, BLK, 512)
    spec = pl.BlockSpec(big, lambda i: (0, 0, i, 0))
    return pl.pallas_call(
        combine_kernel,
        name="combine",
        grid=(own.shape[2] // BLK,),
        in_specs=[spec, spec],
        out_specs=spec,
        out_shape=jax.ShapeDtypeStruct(own.shape, jnp.float32),
        compiler_params=params(),
    )(own, sib)


def body(
    adjoint_old, source_term, face_stream, face_pitch, diag_scale, volume, face_blocks, diag_inverse,
    periodic_block, frequency, phase_shift, periodic_cells, periodic_targets, periodic_weights, periodic_counts,
):
    position = lax.axis_index("inst")
    common = (face_blocks, diag_inverse, frequency, source_term, face_stream, face_pitch, diag_scale, volume)

    parts = [adjoint_old[:, :, b * BLK : (b + n) * BLK] for b, n in SEND]
    first = partner(parts[0], 2)
    out, lo, hi = pick(
        periodic_block, periodic_counts, adjoint_old.reshape(12, 64, 512), face_stream, periodic_cells[0],
        periodic_weights[0],
    )
    out_par = partner(out, 2)
    out_sib = partner(out, 1)
    later = [partner(x, 2) for x in parts[1:]]
    sib0 = partner(adjoint_old, 1)
    halo0 = (from_behind(lo, 1), from_behind(hi, -1))
    out_sp = partner(out_par, 1)

    pool = [(out, position), (out_sib, position ^ 1), (out_par, position ^ 2), (out_sp, position ^ 3)]
    chosen = []
    for j in range(2):
        want = lax.rem(2 * position + j - phase_shift[0] + INSTANCES, INSTANCES)
        value = jnp.zeros((6, 32, 128), jnp.float32)
        for x, home in pool:
            for i in range(2):
                value = jnp.where(want == 2 * home + i, x[i], value)
        chosen.append(value)
    routed = jnp.concatenate(chosen, axis=0).transpose(1, 0, 2)
    arrived = lax.all_to_all(routed, "space", split_axis=0, concat_axis=0, tiled=True)
    targets = periodic_targets[:, 0, :]

    par0 = [first] + later
    sp0 = [partner(x, 1) for x in par0]

    a1, pieces, pers = None, [], []
    edge_lo = edge_hi = None
    for b0, nb in PIECES:
        per = place(arrived, targets, (b0, nb))
        which = [k for k, (s, n) in enumerate(SEND) if s <= b0 and b0 + nb <= s + n][0]
        a1, piece, e_lo, e_hi = sweep(
            False, (b0, nb), common, adjoint_old, halo0, per, sib0, b0, (par0[which], sp0[which]),
            b0 - SEND[which][0], None if a1 is None else (a1,),
        )
        if b0 == 0:
            edge_hi = e_hi
        if b0 + nb == 8:
            edge_lo = e_lo
        sib1 = partner(piece, 1)
        far = partner(combine(piece, sib1), 2)
        pieces.append((b0, nb, sib1, far))
        pers.append(per)
    halo1 = (from_behind(edge_lo, 1), from_behind(edge_hi, -1))
    outs = None
    for (b0, nb, sib1, far), per in zip(pieces, pers):
        outs = sweep(True, (b0, nb), common, a1, halo1, per, sib1, 0, (far,), 0, outs)
    return (outs[0], outs[1])


def solution(mesh):
    in_specs = (
        P("inst", None, "space", None),
        P("inst", None, "space", None),
        P("inst", "space", None),
        P("inst", "space", None),
        P("inst", "space", None),
        P("space", None),
        P(),
        P("inst", None, None),
        P(),
        P(),
        P(),
        P("space", None, None),
        P(None, "space", None),
        P("space", None, None),
        P("space", None),
    )
    out_specs = (P("inst", None, "space", None), P("inst", None, "space", None))
    return jax.shard_map(body, mesh=mesh, in_specs=in_specs, out_specs=out_specs, check_vma=False)
```

```python
import math

import jax
import jax.numpy as jnp
import numpy as np
from jax import lax
from jax.experimental import pallas as pl
from jax.experimental.pallas import tpu as pltpu
from jax.sharding import PartitionSpec as P

INSTANCES = 8
FIELDS = (0, 1, 2, 3, 4, 5, 8, 9, 10, 11, 12, 13)
BLK = 8
EDGE = (0, 2, 7)
PIECES = (EDGE, (1, 3, 1), (4, 3, 1))
VMEM = 40 * 1024 * 1024
MOST = 60 * 1024 * 1024
SMALL = pl.CostEstimate(flops=1024, transcendentals=0, bytes_accessed=4096)


def coef(k):
    k = k % INSTANCES
    if k in (0, 4):
        return 0.0
    return 0.5 * (-1.0) ** k / math.tan(math.pi * k / INSTANCES)


def partner(value, bit):
    return lax.ppermute(value, "inst", [(i, i ^ bit) for i in range(4)])


def halo_pairs(value, odd):
    count = lax.axis_size("space")
    pairs = [(p, p + 1) for p in range(odd, count - 1, 2)]
    return lax.ppermute(value, "space", pairs + [(q, p) for p, q in pairs])


def is_even():
    return lax.rem(lax.axis_index("space"), 2) == 0


def smem():
    return pl.BlockSpec(memory_space=pltpu.SMEM)


def params(limit=VMEM):
    return pltpu.CompilerParams(vmem_limit_bytes=limit)


def split(x):
    hi = x.astype(jnp.bfloat16)
    lo = (x - hi.astype(jnp.float32)).astype(jnp.bfloat16)
    return hi, lo


def pick_kernel(ndest, group, pb_ref, cnt_ref, a_ref, fs_ref, cell_ref, wt_ref, out_ref, lo_ref, hi_ref, tab):
    step = pl.program_id(0)
    even = is_even()

    @pl.when(step == 0)
    def _():
        for f in range(12):
            hi, lo = split(a_ref[f])
            tab[f * 64 : f * 64 + 64, 0:512] = hi
            tab[f * 64 : f * 64 + 64, 512:1024] = lo
        for f in range(12):
            last_row = fs_ref[f // 6, 7:8, :] * a_ref[f, 63:64, :]
            first_row = a_ref[f, 0:1, :]
            lo_ref[f : f + 1, :] = jnp.where(even, last_row, first_row)
            hi_ref[f : f + 1, :] = jnp.where(even, first_row, last_row)

    cells = cell_ref[...]
    cols = lax.bitwise_and(cells, 511)
    rows = lax.shift_right_logical(cells, 9)
    lane = lax.broadcasted_iota(jnp.int32, (512, 128), 0)
    sub = lax.broadcasted_iota(jnp.int32, (64, 128), 0)
    slot = lax.broadcasted_iota(jnp.int32, (1, 128), 1)
    for first in range(0, ndest, group):
        hot = jnp.concatenate(
            [
                jnp.where(lane == cols[q : q + 1, :], 1.0, 0.0).astype(jnp.bfloat16)
                for q in range(first, first + group)
            ],
            axis=1,
        )
        part = jnp.dot(tab[...], jnp.concatenate([hot, hot], axis=0), preferred_element_type=jnp.float32)
        for k in range(group):
            q = first + k
            mask = sub == rows[q : q + 1, :]
            weight = jnp.where(slot < cnt_ref[0, step * ndest + q], wt_ref[q : q + 1, :], 0.0)
            for g in range(2):
                got = []
                for v in range(6):
                    f = g * 6 + v
                    mine = part[f * 64 : f * 64 + 64, k * 128 : k * 128 + 128]
                    got.append(jnp.sum(jnp.where(mask, mine, 0.0), axis=0, keepdims=True))
                for u in range(6):
                    total = pb_ref[0, u] * got[0]
                    for v in range(1, 6):
                        total = total + pb_ref[v, u] * got[v]
                    out_ref[q, 8 * g + u : 8 * g + u + 1, :] = total * weight
                out_ref[q, 8 * g + 6 : 8 * g + 8, :] = jnp.zeros((2, 128), jnp.float32)


def pick(block, counts, a, fs, cells, weights, ndest=32, group=4):
    def kernel(*refs):
        pick_kernel(ndest, group, *refs)

    return pl.pallas_call(
        kernel,
        name="pick",
        grid=(32 // ndest,),
        in_specs=[
            smem(),
            smem(),
            pl.BlockSpec((12, 64, 512), lambda i: (0, 0, 0)),
            pl.BlockSpec((2, 8, 512), lambda i: (0, 7, 0)),
            pl.BlockSpec((ndest, 128), lambda i: (i, 0)),
            pl.BlockSpec((ndest, 128), lambda i: (i, 0)),
        ],
        out_specs=[
            pl.BlockSpec((ndest, 16, 128), lambda i: (i, 0, 0)),
            pl.BlockSpec((12, 512), lambda i: (0, 0)),
            pl.BlockSpec((12, 512), lambda i: (0, 0)),
        ],
        out_shape=[
            jax.ShapeDtypeStruct((32, 16, 128), jnp.float32),
            jax.ShapeDtypeStruct((12, 512), jnp.float32),
            jax.ShapeDtypeStruct((12, 512), jnp.float32),
        ],
        scratch_shapes=[pltpu.VMEM((768, 1024), jnp.bfloat16)],
        cost_estimate=SMALL,
        compiler_params=params(),
    )(block, counts, a, fs, cells, weights)


def pack_kernel(head, tail, out):
    out[:, :, 0:BLK, :] = head[...]
    out[:, :, BLK : 2 * BLK, :] = tail[...]


def pack(a):
    big = (2, 6, BLK, 512)
    return pl.pallas_call(
        pack_kernel,
        name="pack",
        grid=(1,),
        in_specs=[pl.BlockSpec(big, lambda i: (0, 0, 0, 0)), pl.BlockSpec(big, lambda i: (0, 0, 7, 0))],
        out_specs=pl.BlockSpec((2, 6, 2 * BLK, 512), lambda i: (0, 0, 0, 0)),
        out_shape=jax.ShapeDtypeStruct((2, 6, 2 * BLK, 512), jnp.float32),
        cost_estimate=SMALL,
        compiler_params=params(MOST),
    )(a, a)


def rows_of(a, piece):
    return a[:, :, piece[0] * BLK : (piece[0] + piece[1]) * BLK]


def route_kernel(shift_ref, own, sib, par, sp, out):
    position = lax.axis_index("inst")
    core = lax.rem(position, 2)
    chip = position - core
    sibling = chip + 1 - core
    far = 2 - chip
    homes = [position, sibling, far + core, far + 1 - core]
    for j in range(2):
        want = lax.rem(2 * position + j - shift_ref[0] + INSTANCES, INSTANCES)
        value = jnp.zeros((32, 8, 128), jnp.float32)
        for x, home in zip((own, sib, par, sp), homes):
            for i in range(2):
                value = jnp.where(want == 2 * home + i, x[:, 8 * i : 8 * i + 8, :], value)
        out[:, 8 * j : 8 * j + 8, :] = value


def route(shift, pieces):
    return pl.pallas_call(
        route_kernel,
        name="route",
        in_specs=[smem()] + [pl.BlockSpec(memory_space=pltpu.VMEM)] * 4,
        out_specs=pl.BlockSpec(memory_space=pltpu.VMEM),
        out_shape=jax.ShapeDtypeStruct((32, 16, 128), jnp.float32),
        cost_estimate=SMALL,
        compiler_params=params(),
    )(shift, *pieces)


def place_kernel(piece, ndest, val_ref, tgt_ref, out_ref):
    b0, nb, st = piece
    rows_here = nb * BLK
    step = pl.program_id(0)
    cells = tgt_ref[...]
    cols = lax.bitwise_and(cells, 511)
    rows = lax.shift_right_logical(cells, 9)
    if st == 1:
        rows = rows - b0 * BLK
    else:
        jump = (st - 1) * BLK
        rows = jnp.where(rows < BLK, rows, jnp.where(rows >= st * BLK, rows - jump, -1))
    lane = lax.broadcasted_iota(jnp.int32, (512, 128), 0)
    sub = lax.broadcasted_iota(jnp.int32, (rows_here, 128), 0)
    hot = jnp.concatenate(
        [jnp.where(lane == cols[p : p + 1, :], 1.0, 0.0).astype(jnp.bfloat16) for p in range(ndest)], axis=1
    )
    highs, lows = [], []
    for p in range(ndest):
        mask = sub == rows[p : p + 1, :]
        spread = [jnp.where(mask, val_ref[p, f : f + 1, :], 0.0) for f in FIELDS]
        hi, lo = split(jnp.concatenate(spread, axis=0))
        highs.append(hi)
        lows.append(lo)
    both = jnp.concatenate([jnp.concatenate(highs, axis=1), jnp.concatenate(lows, axis=1)], axis=0)
    total = lax.dot_general(both, hot, (((1,), (1,)), ((), ())), preferred_element_type=jnp.float32)
    total = (total[: 12 * rows_here] + total[12 * rows_here :]).reshape(12, rows_here, 512)
    if ndest == 32:
        out_ref[...] = total
        return

    @pl.when(step == 0)
    def _():
        out_ref[...] = total

    @pl.when(step > 0)
    def _():
        out_ref[...] += total


def place(values, targets, piece, ndest):
    rows = piece[1] * BLK

    def kernel(*refs):
        place_kernel(piece, ndest, *refs)

    return pl.pallas_call(
        kernel,
        name="place",
        grid=(32 // ndest,),
        in_specs=[
            pl.BlockSpec((ndest, 16, 128), lambda i: (i, 0, 0)),
            pl.BlockSpec((ndest, 128), lambda i: (i, 0)),
        ],
        out_specs=pl.BlockSpec((12, rows, 512), lambda i: (0, 0, 0)),
        out_shape=jax.ShapeDtypeStruct((12, rows, 512), jnp.float32),
        cost_estimate=SMALL,
        compiler_params=params(),
    )(values, targets)


def own_terms(core, j):
    own = [coef(i - j) for i in range(2)]
    sib = [(coef(2 + i - j), coef(-2 + i - j)) for i in range(2)]
    return own, [jnp.where(core == 0, jnp.float32(e), jnp.float32(o)) for e, o in sib]


def far_terms(core, j):
    par = [coef(4 + i - j) for i in range(2)]
    sp = [(coef(6 + i - j), coef(2 + i - j)) for i in range(2)]
    return par, [jnp.where(core == 0, jnp.float32(e), jnp.float32(o)) for e, o in sp]


def weighted(terms, fields):
    total = None
    for c, x in zip(terms, fields):
        if isinstance(c, float) and c == 0.0:
            continue
        total = c * x if total is None else total + c * x
    return total


def sweep_kernel(
    last_sweep, piece, nfar, cf_ref, fr_ref, cur, prev, nxt, hlo, hhi, src, fs_ref, fsp_ref, fp_ref, dg_ref,
    vol_ref, per_ref, sib, *rest,
):
    blk = piece[0] + piece[2] * pl.program_id(0)
    edge = piece == EDGE
    even = is_even()
    core = lax.rem(lax.axis_index("inst"), 2)
    far, rest = rest[:nfar], rest[nfar:]
    if last_sweep:
        out, res_out = rest[-2:]
    elif edge:
        out, copy, edge_lo, edge_hi = rest[-4:]
    else:
        out, copy = rest[-2:]
    row = lax.broadcasted_iota(jnp.int32, (BLK, 512), 0)
    col = lax.broadcasted_iota(jnp.int32, (BLK, 512), 1)
    top, bottom = row == 0, row == BLK - 1
    left, right = col == 0, col == 511
    fv = fr_ref[0] * vol_ref[...]
    for g in range(2):
        fs, fp, dg = fs_ref[g], fp_ref[g], dg_ref[g]
        fs_before = fsp_ref[g, BLK - 1 : BLK, :]
        own_w, sib_w = own_terms(core, g)
        if nfar == 2:
            par_w, sp_w = far_terms(core, g)
        r = [src[g, u] - per_ref[g * 6 + u] for u in range(6)]
        for v in range(6):
            f = g * 6 + v
            a = cur[g, v]
            before = fs_before * prev[g, v, BLK - 1 : BLK, :]
            after = nxt[g, v, 0:1, :]
            if edge:
                one, two = hlo[f : f + 1, :], hhi[f : f + 1, :]
                before = jnp.where(blk == 0, jnp.where(even, two, one), before)
                after = jnp.where(blk == 7, jnp.where(even, one, two), after)
            lower = jnp.where(top, before, pltpu.roll(fs * a, 1, 0))
            upper = fs * jnp.where(bottom, after, pltpu.roll(a, BLK - 1, 0))
            lft = jnp.where(left, 0.0, pltpu.roll(fp * a, 1, 1))
            rgt = fp * jnp.where(right, 0.0, pltpu.roll(a, 511, 1))
            for u in range(6):
                r[u] = r[u] - (
                    (cf_ref[0, v, u] * lower + cf_ref[1, v, u] * upper)
                    + (cf_ref[2, v, u] * lft + cf_ref[3, v, u] * rgt)
                )
            mixed = weighted(own_w + sib_w, [cur[0, v], cur[1, v], sib[0, v], sib[1, v]])
            if nfar == 2:
                par, sp = far
                mixed = mixed + weighted(par_w + sp_w, [par[0, v], par[1, v], sp[0, v], sp[1, v]])
            else:
                mixed = mixed + far[0][g, v]
            r[v] = r[v] - fv * mixed
        for u in range(6):
            total = cf_ref[4 + g, u, 0] * r[0]
            for v in range(1, 6):
                total = total + cf_ref[4 + g, u, v] * r[v]
            new = dg * total
            out[g, u] = new
            if last_sweep:
                res_out[g, u] = r[u]
            else:
                copy[g, u] = new
                if edge:
                    f = g * 6 + u

                    last_row = (fs * new)[BLK - 1 : BLK, :]
                    first_row = new[0:1, :]

                    @pl.when(jnp.logical_and(blk == 7, even))
                    def _(row=last_row, f=f):
                        edge_lo[f : f + 1, :] = row

                    @pl.when(jnp.logical_and(blk == 7, jnp.logical_not(even)))
                    def _(row=last_row, f=f):
                        edge_hi[f : f + 1, :] = row

                    @pl.when(jnp.logical_and(blk == 0, even))
                    def _(row=first_row, f=f):
                        edge_hi[f : f + 1, :] = row

                    @pl.when(jnp.logical_and(blk == 0, jnp.logical_not(even)))
                    def _(row=first_row, f=f):
                        edge_lo[f : f + 1, :] = row


def sweep(last_sweep, piece, common, a, halo, per, per_off, sib, sib_at, far, far_off, into):
    b0, nb, st = piece
    coefs, fr, src, fs, fp, dg, vol = common
    big = (2, 6, BLK, 512)
    small = (2, BLK, 512)

    def blk(i):
        return b0 + st * i

    def low(i):
        return jnp.maximum(blk(i) - 1, 0)

    def high(i):
        return jnp.minimum(blk(i) + 1, 7)

    def here(off):
        return pl.BlockSpec(big, lambda i: (0, 0, off + i, 0))

    whole = pl.BlockSpec(big, lambda i: (0, 0, blk(i), 0))
    halo_spec = pl.BlockSpec((12, 512), lambda i: (0, 0))
    specs = [
        smem(), smem(),
        whole,
        pl.BlockSpec(big, lambda i: (0, 0, low(i), 0)),
        pl.BlockSpec(big, lambda i: (0, 0, high(i), 0)),
        halo_spec, halo_spec,
        whole,
        pl.BlockSpec(small, lambda i: (0, blk(i), 0)),
        pl.BlockSpec(small, lambda i: (0, low(i), 0)),
        pl.BlockSpec(small, lambda i: (0, blk(i), 0)),
        pl.BlockSpec(small, lambda i: (0, blk(i), 0)),
        pl.BlockSpec((BLK, 512), lambda i: (blk(i), 0)),
        pl.BlockSpec((12, BLK, 512), lambda i: (0, per_off + i, 0)),
        whole if sib_at is None else here(sib_at),
    ]
    args = [coefs, fr, a, a, a, halo[0], halo[1], src, fs, fs, fp, dg, vol, per, sib]
    for x in far:
        specs.append(here(far_off))
        args.append(x)
    full = jax.ShapeDtypeStruct((2, 6, 64, 512), jnp.float32)
    out_specs, out_shape = [whole], [full]
    if last_sweep:
        out_specs.append(whole)
        out_shape.append(full)
    else:
        out_specs.append(here(0))
        out_shape.append(jax.ShapeDtypeStruct((2, 6, nb * BLK, 512), jnp.float32))
        if piece == EDGE:
            out_specs += [halo_spec, halo_spec]
            out_shape += [jax.ShapeDtypeStruct((12, 512), jnp.float32)] * 2
    aliases = {}
    for k, x in enumerate(into):
        aliases[len(args)] = k
        specs.append(pl.BlockSpec(memory_space=pl.ANY))
        args.append(x)

    def kernel(*refs):
        sweep_kernel(last_sweep, piece, len(far), *refs)

    return pl.pallas_call(
        kernel,
        name="sweep2" if last_sweep else "sweep1",
        grid=(nb,),
        in_specs=specs,
        out_specs=out_specs,
        out_shape=out_shape,
        input_output_aliases=aliases,
        cost_estimate=SMALL,
        compiler_params=params(),
    )(*args)


def body(
    adjoint_old, source_term, face_stream, face_pitch, diag_scale, volume, face_blocks, diag_inverse,
    periodic_block, frequency, phase_shift, periodic_cells, periodic_targets, periodic_weights, periodic_counts,
):
    barrier = lax.optimization_barrier

    first, second, third = PIECES

    edge_rows = pack(adjoint_old)
    par_first = partner(edge_rows, 2)
    early, _ = barrier((adjoint_old, edge_rows))
    rows2 = rows_of(early, second)
    par_second = partner(rows2, 2)
    early, _ = barrier((adjoint_old, rows2))
    out, lo, hi = pick(
        periodic_block, periodic_counts, early.reshape(12, 64, 512), face_stream, periodic_cells[0],
        periodic_weights[0],
    )
    out, par_first = barrier((out, par_first))
    arrived0 = lax.all_to_all(out, "space", split_axis=0, concat_axis=0, tiled=True)
    rows3, lo, hi, fb, di, _ = barrier((adjoint_old, lo, hi, face_blocks, diag_inverse, out))
    coefs = jnp.concatenate([fb, di], axis=0)
    halo0 = (halo_pairs(lo, 0), halo_pairs(hi, 1))
    rows3 = rows_of(rows3, third)
    arrived0, halo0, coefs = barrier((arrived0, halo0, coefs))
    common = (coefs, frequency, source_term, face_stream, face_pitch, diag_scale, volume)
    arrived_sib = partner(arrived0, 1)
    arrived_par = partner(arrived0, 2)
    rows3, arrived_par = barrier((rows3, arrived_par))
    par_third = partner(rows3, 2)
    arrived_sp = partner(arrived_par, 1)
    arrived = route(phase_shift, (arrived0, arrived_sib, arrived_par, arrived_sp))
    own, par_first, par_second, _ = barrier((adjoint_old, par_first, par_second, arrived0))
    sib0 = partner(own, 1)
    sp_first = partner(par_first, 1)
    sp_second = partner(par_second, 1)
    targets = periodic_targets[:, 0, :]

    per_first = place(arrived, targets, first, 32)
    a1, piece1, lo1, hi1 = sweep(
        False, first, common, adjoint_old, halo0, per_first, 0, sib0, None, (par_first, sp_first), 0, ()
    )
    par1_first = partner(piece1, 2)
    arrived2, _ = barrier((arrived, piece1))
    per_second = place(arrived2, targets, second, 32)
    a1, piece2 = sweep(
        False, second, common, adjoint_old, halo0, per_second, 0, sib0, None, (par_second, sp_second), 0, (a1,)
    )
    halo1 = (halo_pairs(lo1, 0), halo_pairs(hi1, 1))
    sent2, par1_first, halo1 = barrier((piece2, par1_first, halo1))
    par1_second = partner(sent2, 2)
    par_third, arrived3, _ = barrier((par_third, arrived, par1_first))
    sp_third = partner(par_third, 1)
    per_third = place(arrived3, targets, third, 16)
    a1, piece3 = sweep(
        False, third, common, adjoint_old, halo0, per_third, 0, sib0, None, (par_third, sp_third), 0, (a1,)
    )
    sent3, par1_second = barrier((piece3, par1_second))
    par1_third = partner(sent3, 2)
    piece1, piece2, _ = barrier((piece1, piece2, sent3))
    sib1_third = partner(piece3, 1)
    sib1_first = partner(piece1, 1)
    sib1_second = partner(piece2, 1)
    sp1_first = partner(par1_first, 1)
    sp1_second = partner(par1_second, 1)

    outs = sweep(True, second, common, a1, halo1, per_second, 0, sib1_second, 0, (par1_second, sp1_second), 0, ())
    outs = sweep(True, first, common, a1, halo1, per_first, 0, sib1_first, 0, (par1_first, sp1_first), 0, outs)
    par1_third, outs = barrier((par1_third, tuple(outs)))
    sp1_third = partner(par1_third, 1)
    outs = sweep(True, third, common, a1, halo1, per_third, 0, sib1_third, 0, (par1_third, sp1_third), 0, outs)
    return (outs[0], outs[1])


def solution(mesh):
    in_specs = (
        P("inst", None, "space", None),
        P("inst", None, "space", None),
        P("inst", "space", None),
        P("inst", "space", None),
        P("inst", "space", None),
        P("space", None),
        P(),
        P("inst", None, None),
        P(),
        P(),
        P(),
        P("space", None, None),
        P(None, "space", None),
        P("space", None, None),
        P("space", None),
    )
    out_specs = (P("inst", None, "space", None), P("inst", None, "space", None))
    return jax.shard_map(body, mesh=mesh, in_specs=in_specs, out_specs=out_specs, check_vma=False)
```
